32 devices in a mesh: blk: 8 (over y, x, core), team: 4 (over z).
Axes of the slice: x: 2, y: 2, z: 4, core: 2. Of those that a mesh axis runs over, the one named last changes fastest.
Arguments:
- features: bfloat16 [8192, 128], P(('blk', 'team')), may hold values from -0.796875 to 0.796875
- left_vectors: bfloat16 [8192, 128], P(('blk', 'team')), may hold values from -0.8984375 to 0.8984375
- right_vectors: bfloat16 [8192, 128], P(('blk', 'team')), may hold values from -0.8984375 to 0.8984375
Outputs:
- feature_grad: float32 [8192, 128], P(('blk', 'team'))
The draws below stay inside these ranges and needn't reach their ends.
All inputs are finite; a program needn't handle non-finite values.
Results may differ from the reference program's by a relative error of at most 0.0039.
Values may be sent and summed in bfloat16 or wider, within the bound.
A program may use at most 64 MiB of HBM per device.

```python
import jax
import jax.numpy as jnp
from jax import lax

FEAT = 128
VEC = 128
POINTS = 8192


def steps_of(own_key, dims, pieces, least, high):
    gain, own = 1.0, jax.random.fold_in(own_key, 6)
    for position, parts in pieces:
        draws = jnp.exp(jax.random.uniform(jax.random.fold_in(own, position), (parts,), jnp.float32, least / len(pieces), high / len(pieces)))
        gain = gain * jnp.repeat(draws, dims[position] // parts).reshape([-1 if axis == position else 1 for axis in range(len(dims))])
    return gain


def normal_values(rng, dims, scale, reach, shards=(), kind=jnp.bfloat16):
    factor_of = steps_of(rng, dims, shards, -0.22, 0.18) if shards else 1.0
    drawn = jax.random.normal(rng, dims, jnp.float32) * scale * factor_of
    return jnp.minimum(jnp.maximum(drawn, -reach), reach).astype(kind)


def setup_inputs(seed: int = 0) -> dict:
    splits = jax.random.split(jax.random.key(seed), 4)
    return {
        "features": normal_values(splits[0], (POINTS, FEAT), 0.1, 0.796875, ((0, 32),)),
        "left_vectors": normal_values(splits[1], (POINTS, VEC), 0.11, 0.8984375, ((0, 32),)),
        "right_vectors": normal_values(splits[2], (POINTS, VEC), 0.11, 0.8984375, ((0, 32),)),
    }


def pair_block(target_x, target_l, target_r, target_norm, source_x, source_l, source_r, source_norm):
    cross = jnp.dot(target_x, source_x.T, preferred_element_type=jnp.float32)
    dist_sq = target_norm[:, None] + source_norm[None, :] - 2.0 * cross
    radius = jnp.sqrt(jnp.maximum(dist_sq, 0.0))
    couple = jnp.dot(target_l, source_r.T, preferred_element_type=jnp.float32) + jnp.dot(target_r, source_l.T, preferred_element_type=jnp.float32)
    root_five = jnp.float32(5.0) ** 0.5
    weight = (-(5.0 / 3.0) * (1.0 + root_five * radius) * jnp.exp(-root_five * radius) * couple).astype(jnp.bfloat16)
    row_total = lax.optimization_barrier(jnp.sum(weight.astype(jnp.float32), axis=1))
    return row_total[:, None] * target_x.astype(jnp.float32) - jnp.dot(weight, source_x, preferred_element_type=jnp.float32)

def reference(features, left_vectors, right_vectors):
    total = features.shape[0]
    width = min(512, total)
    norms = lax.optimization_barrier(jnp.sum(features.astype(jnp.float32) ** 2, axis=1))
    count_blocks = total // width

    def one_block(packed):
        block_x, block_l, block_r, block_norm = packed
        return pair_block(block_x, block_l, block_r, block_norm, features, left_vectors, right_vectors, norms)
    result = lax.map(one_block, (features.reshape(count_blocks, width, -1), left_vectors.reshape(count_blocks, width, -1), right_vectors.reshape(count_blocks, width, -1), norms.reshape(count_blocks, width)))
    return result.reshape(total, -1)
```

```python
import functools
import math

import jax
import jax.numpy as jnp
from jax import lax
from jax.experimental import pallas as pl
from jax.experimental.pallas import tpu as pltpu
from jax.sharding import PartitionSpec as P

MESH = pl.DeviceIdType.MESH
LOG2E = math.log2(math.e)
RATE = math.sqrt(5.0) * LOG2E
GAIN = -(5.0 / 3.0) / LOG2E
NT = (((1,), (1,)), ((), ()))


def flip(index, bits):
    step = 1
    while step <= bits:
        if bits & step:
            index = index + step - 2 * step * ((index // step) % 2)
        step *= 2
    return index


def columns(norm, lane, first, ones):
    high = norm.astype(jnp.bfloat16).astype(jnp.float32)
    rest = norm - high
    mid = rest.astype(jnp.bfloat16).astype(jnp.float32)
    low = rest - mid
    out = jnp.where((lane >= ones) & (lane < ones + 3), 1.0, 0.0)
    for place, term in enumerate((high, mid, low)):
        out = jnp.where(lane == first + place, term, out)
    return out.astype(jnp.bfloat16)


def kernel(
    planes, teams, tile, x_hbm, l_hbm, r_hbm, out_ref,
    own, tgt, src, tgt_aug, src_aug, acc, grad_out, grad_in,
    load_sem, tgt_send, tgt_recv, z_send, z_recv, p_send, p_recv, g_send, g_recv,
):
    blk, team = lax.axis_index("blk"), lax.axis_index("team")
    plane, core = blk // 2, blk % 2
    rows, feat = x_hbm.shape

    loads = [
        pltpu.make_async_copy(ref, own.at[i], load_sem.at[i])
        for i, ref in enumerate((x_hbm, l_hbm, r_hbm))
    ]
    for load in loads:
        load.start()

    partner = (plane * 2 + 1 - core, team)
    plane_peer = [(flip(plane, k) * 2 + core, team) for k in range(planes)]
    team_peer = [(blk, flip(team, k)) for k in range(teams)]
    peers = [partner] + plane_peer[1:] + team_peer[1:]
    barrier = pltpu.get_barrier_semaphore()
    for peer in peers:
        pl.semaphore_signal(barrier, inc=1, device_id=peer, device_id_type=MESH)

    def remote(source, target, send, recv, peer):
        return pltpu.make_async_remote_copy(
            src_ref=source, dst_ref=target, send_sem=send, recv_sem=recv,
            device_id=peer, device_id_type=MESH,
        )

    to_plane = [None] + [
        remote(own, tgt.at[k - 1], tgt_send.at[k], tgt_recv.at[k], plane_peer[k])
        for k in range(1, planes)
    ]
    to_team = [None] + [
        remote(own, src.at[2 * k], z_send.at[k], z_recv.at[k], team_peer[k])
        for k in range(1, teams)
    ]
    to_partner = [
        remote(own if k == 0 else src.at[2 * k], src.at[2 * k + 1], p_send.at[k], p_recv.at[k], partner)
        for k in range(teams)
    ]
    to_owner = [None] + [
        remote(grad_out.at[k - 1], grad_in.at[k - 1], g_send.at[k], g_recv.at[k], plane_peer[k])
        for k in range(1, planes)
    ]

    for load in loads:
        load.wait()
    pl.semaphore_wait(barrier, len(peers))
    to_partner[0].start()
    for k in range(1, teams):
        to_team[k].start()
    for k in range(1, planes):
        to_plane[k].start()

    def norm_of(ref):
        x = ref[0]
        xf = x.astype(jnp.float32)
        return x, jnp.sum(xf * xf, axis=1, keepdims=True)

    lane = lax.broadcasted_iota(jnp.int32, (rows, feat), 1)

    def raw_target(k):
        return own if k == 0 else tgt.at[k - 1]

    def raw_source(s):
        return own if s == 0 else src.at[s]

    def prepare_target(k):
        x, norm = norm_of(raw_target(k))
        tgt_aug[k, :, :feat] = x * jnp.bfloat16(-2.0)
        tgt_aug[k, :, feat:] = columns(norm, lane, 0, 3)

    def prepare_source(s):
        x, norm = norm_of(raw_source(s))
        src_aug[s, :, :feat] = x
        src_aug[s, :, feat:] = columns(norm, lane, 3, 0)

    def tile_pair(k, s, i, j, first):
        ti, sj = pl.ds(i, tile), pl.ds(j, tile)
        target, source = raw_target(k), raw_source(s)
        src_a = src_aug[s, sj, :]
        dist = lax.dot_general(tgt_aug[k, ti, :], src_a, NT, preferred_element_type=jnp.float32)
        couple = lax.dot_general(
            jnp.concatenate([target[1, ti, :], target[2, ti, :]], axis=1),
            jnp.concatenate([source[2, sj, :], source[1, sj, :]], axis=1),
            NT, preferred_element_type=jnp.float32,
        )
        dist = jnp.maximum(dist, 1e-30)
        power = dist * lax.rsqrt(dist) * (-RATE)
        weight = ((LOG2E - power) * jnp.exp2(power) * couple).astype(jnp.bfloat16)
        part = jnp.dot(weight, src_a, preferred_element_type=jnp.float32)
        if first:
            acc[k, ti, :] = part
        else:
            acc[k, ti, :] += part

    blocks = rows // tile

    def pair(k, s):
        if blocks == 1:
            tile_pair(k, s, 0, 0, s == 0)
            return

        @pl.loop(0, blocks)
        def _(i):
            i = pl.multiple_of(i * tile, tile)
            tile_pair(k, s, i, 0, s == 0)

            @pl.loop(1, blocks)
            def _(j):
                tile_pair(k, s, i, pl.multiple_of(j * tile, tile), False)

    def gradient(k):
        total = acc[k]
        x = raw_target(k)[0].astype(jnp.float32)
        return GAIN * (total[:, feat:feat + 1] * x - total[:, :feat])

    prepare_target(0)
    prepare_source(0)
    pair(0, 0)
    to_partner[0].wait_recv()
    prepare_source(1)
    pair(0, 1)
    if teams > 1:
        to_team[1].wait_recv()
        to_partner[1].start()
    for k in range(1, planes):
        to_plane[k].wait_recv()
        prepare_target(k)
        pair(k, 0)
        pair(k, 1)
    for z in range(1, teams):
        if z > 1:
            to_team[z].wait_recv()
            to_partner[z].start()
        prepare_source(2 * z)
        for k in range(planes):
            pair(k, 2 * z)
        to_partner[z].wait_recv()
        prepare_source(2 * z + 1)
        if z < teams - 1:
            for k in range(planes):
                pair(k, 2 * z + 1)
    for k in reversed(range(planes)):
        if teams > 1:
            pair(k, 2 * teams - 1)
        if k:
            grad_out[k - 1] = gradient(k).astype(jnp.bfloat16)
            to_owner[k].start()
    total = gradient(0)
    for k in reversed(range(1, planes)):
        to_owner[k].wait_recv()
        total += grad_in[k - 1].astype(jnp.float32)
    out_ref[...] = total
    for copy in to_plane[1:] + to_team[1:] + to_partner + to_owner[1:]:
        copy.wait_send()


def local(planes, teams, features, left_vectors, right_vectors):
    rows, feat = features.shape
    kind = jnp.bfloat16
    dma = pltpu.SemaphoreType.DMA
    tile = min(rows, 256)
    return pl.pallas_call(
        functools.partial(kernel, planes, teams, tile),
        out_shape=jax.ShapeDtypeStruct((rows, feat), jnp.float32),
        in_specs=[pl.BlockSpec(memory_space=pl.ANY)] * 3,
        out_specs=pl.BlockSpec(memory_space=pltpu.VMEM),
        scratch_shapes=[
            pltpu.VMEM((3, rows, feat), kind),
            pltpu.VMEM((max(planes - 1, 1), 3, rows, feat), kind),
            pltpu.VMEM((2 * teams, 3, rows, feat), kind),
            pltpu.VMEM((planes, rows, 2 * feat), kind),
            pltpu.VMEM((2 * teams, rows, 2 * feat), kind),
            pltpu.VMEM((planes, rows, 2 * feat), jnp.float32),
            pltpu.VMEM((max(planes - 1, 1), rows, feat), kind),
            pltpu.VMEM((max(planes - 1, 1), rows, feat), kind),
            dma((3,)),
            dma((planes,)), dma((planes,)),
            dma((teams,)), dma((teams,)),
            dma((teams,)), dma((teams,)),
            dma((planes,)), dma((planes,)),
        ],
        compiler_params=pltpu.CompilerParams(collective_id=0, has_side_effects=True),
    )(features, left_vectors, right_vectors)


def solution(mesh):
    spec = P(("blk", "team"), None)
    planes, teams = mesh.shape["blk"] // 2, mesh.shape["team"]
    return jax.shard_map(
        functools.partial(local, planes, teams), mesh=mesh,
        in_specs=(spec, spec, spec), out_specs=spec, check_vma=False,
    )
```

```python
import functools
import math

import jax
import jax.numpy as jnp
from jax import lax
from jax.experimental import pallas as pl
from jax.experimental.pallas import tpu as pltpu
from jax.sharding import PartitionSpec as P

MESH = pl.DeviceIdType.MESH
LOG2E = math.log2(math.e)
RATE = math.sqrt(5.0) * LOG2E
GAIN = -(5.0 / 3.0) / LOG2E
NT = (((1,), (1,)), ((), ()))


def flip(index, bits):
    step = 1
    while step <= bits:
        if bits & step:
            index = index + step - 2 * step * ((index // step) % 2)
        step *= 2
    return index


def columns(norm, lane, first, ones):
    high = norm.astype(jnp.bfloat16).astype(jnp.float32)
    rest = norm - high
    mid = rest.astype(jnp.bfloat16).astype(jnp.float32)
    low = rest - mid
    out = jnp.where((lane >= ones) & (lane < ones + 3), 1.0, 0.0)
    for place, term in enumerate((high, mid, low)):
        out = jnp.where(lane == first + place, term, out)
    return out.astype(jnp.bfloat16)


def kernel(
    planes, teams, tile, split, x_hbm, l_hbm, r_hbm, out_ref,
    own, tgt, src, tgt_aug, src_aug, acc, grad_out, grad_in,
    load_sem, tgt_send, tgt_recv, z_send, z_recv, p_send, p_recv, g_send, g_recv,
):
    blk, team = lax.axis_index("blk"), lax.axis_index("team")
    plane, core = blk // 2, blk % 2
    rows, feat = x_hbm.shape

    loads = [
        pltpu.make_async_copy(ref, own.at[i], load_sem.at[i])
        for i, ref in enumerate((x_hbm, l_hbm, r_hbm))
    ]
    for load in loads:
        load.start()

    partner = (plane * 2 + 1 - core, team)
    plane_peer = [(flip(plane, k) * 2 + core, team) for k in range(planes)]
    peers = [partner] + plane_peer[1:]
    barrier = pltpu.get_barrier_semaphore()
    for peer in peers:
        pl.semaphore_signal(barrier, inc=1, device_id=peer, device_id_type=MESH)
    for step in (1, -1):
        @pl.when((team + step >= 0) & (team + step < teams))
        def _():
            pl.semaphore_signal(barrier, inc=1, device_id=(blk, team + step), device_id_type=MESH)

    def remote(source, target, send, recv, peer):
        return pltpu.make_async_remote_copy(
            src_ref=source, dst_ref=target, send_sem=send, recv_sem=recv,
            device_id=peer, device_id_type=MESH,
        )

    to_plane = [None] + [
        remote(own, tgt.at[k - 1], tgt_send.at[k], tgt_recv.at[k], plane_peer[k])
        for k in range(1, planes)
    ]
    size = rows // split
    left, right = team, teams - 1 - team
    both = jnp.minimum(left, right)

    def position(n):
        paired = n <= 2 * both
        far = jnp.where(paired, (n + 1) // 2, n - both)
        sign = jnp.where(paired, 1 - 2 * (n % 2), jnp.where(left < right, 1, -1))
        return team + sign * far, -sign

    order = [None] + [position(n) for n in range(1, teams)]

    def part_of(ref, h):
        return ref.at[:, pl.ds(h * size, size)]

    def line_copy(source, shard, h, send, step):
        return remote(
            part_of(source, h), part_of(src.at[2 * shard], h), send, z_recv.at[shard, h],
            (blk, team + step),
        )

    def can_go(step):
        return (team + step >= 0) & (team + step < teams)

    def own_copy(step, h):
        return line_copy(own, team, h, z_send.at[team if step > 0 else teams, h], step)

    def forward(n, h):
        shard, step = order[n]
        return line_copy(src.at[2 * shard], shard, h, z_send.at[shard, h], step)

    def relay(n, h):
        shard = order[n][0]
        return remote(
            part_of(src.at[2 * shard], h), part_of(src.at[2 * shard + 1], h),
            p_send.at[shard, h], p_recv.at[shard, h], partner,
        )

    mine = 2 * team
    to_partner = remote(own, src.at[mine + 1], p_send.at[team, 0], p_recv.at[team, 0], partner)
    to_owner = [None] + [
        remote(grad_out.at[k - 1], grad_in.at[k - 1], g_send.at[k], g_recv.at[k], plane_peer[k])
        for k in range(1, planes)
    ]

    for load in loads:
        load.wait()
    on_line = jnp.minimum(team, 1) + jnp.minimum(teams - 1 - team, 1)
    pl.semaphore_wait(barrier, len(peers) + on_line)
    to_partner.start()
    for h in range(split):
        for step in (1, -1):
            @pl.when(can_go(step))
            def _():
                own_copy(step, h).start()
    for k in range(1, planes):
        to_plane[k].start()

    def norm_of(x):
        xf = x.astype(jnp.float32)
        return jnp.sum(xf * xf, axis=1, keepdims=True)


    def raw_target(k):
        return own if k == 0 else tgt.at[k - 1]

    def raw_source(s):
        return own if s is mine else src.at[s]

    lane = lax.broadcasted_iota(jnp.int32, (rows, feat), 1)

    def prepare_target(k):
        x = raw_target(k)[0]
        tgt_aug[k, :, :feat] = x * jnp.bfloat16(-2.0)
        tgt_aug[k, :, feat:] = columns(norm_of(x), lane, 0, 3)

    def prepare_source(s):
        x = raw_source(s)[0]
        src_aug[s, :, :feat] = x
        src_aug[s, :, feat:] = columns(norm_of(x), lane, 3, 0)

    def tile_pair(k, s, i, j, first):
        ti, sj = pl.ds(i, tile), pl.ds(j, tile)
        target, source = raw_target(k), raw_source(s)
        src_a = src_aug[s, sj, :]
        dist = lax.dot_general(tgt_aug[k, ti, :], src_a, NT, preferred_element_type=jnp.float32)
        couple = lax.dot_general(
            jnp.concatenate([target[1, ti, :], target[2, ti, :]], axis=1),
            jnp.concatenate([source[2, sj, :], source[1, sj, :]], axis=1),
            NT, preferred_element_type=jnp.float32,
        )
        dist = jnp.maximum(dist, 1e-30)
        power = dist * lax.rsqrt(dist) * (-RATE)
        weight = ((LOG2E - power) * jnp.exp2(power) * couple).astype(jnp.bfloat16)
        part = jnp.dot(weight, src_a, preferred_element_type=jnp.float32)
        if first:
            acc[k, ti, :] = part
        else:
            acc[k, ti, :] += part

    def pair(k, s):
        if rows == tile:
            tile_pair(k, s, 0, 0, s is mine)
            return

        @pl.loop(0, rows // tile)
        def _(i):
            i = pl.multiple_of(i * tile, tile)
            tile_pair(k, s, i, 0, s is mine)

            @pl.loop(1, rows // tile)
            def _(j):
                tile_pair(k, s, i, pl.multiple_of(j * tile, tile), False)

    def gradient(k):
        total = acc[k]
        x = raw_target(k)[0].astype(jnp.float32)
        return GAIN * (total[:, feat:feat + 1] * x - total[:, :feat])

    inner = both > 0

    def receive(n, h):
        line_copy(own, order[n][0], h, z_send.at[0, 0], 0).wait_recv()

        @pl.when(can_go(order[n][1]))
        def _():
            forward(n, h).start()
        relay(n, h).start()

    def receive_when(condition, n, halves=range(split)):
        if n < teams:
            @pl.when(condition)
            def _():
                for h in halves:
                    receive(n, h)

    def take(n):
        prepare_source(2 * order[n][0])
        return 2 * order[n][0]

    def take_partner(n):
        for h in range(split):
            relay(n, h).wait_recv()
        prepare_source(2 * order[n][0] + 1)
        return 2 * order[n][0] + 1

    prepare_target(0)
    prepare_source(mine)
    pair(0, mine)
    to_partner.wait_recv()
    next_door = mine + 1
    prepare_source(next_door)
    pair(0, next_door)
    if teams > 1:
        for h in range(split):
            receive(1, h)
        receive_when(inner, 2)
        first = take(1)
        pair(0, first)
    for k in range(1, planes):
        to_plane[k].wait_recv()
        if k == planes - 1:
            receive_when(inner, 3)
        prepare_target(k)
        pair(k, mine)
        pair(k, next_door)
        if teams > 1:
            pair(k, first)
    outer = jnp.logical_not(inner)
    receive_when(outer, 2)
    for n in range(1, teams - 1):
        slot = take_partner(n)
        for k in range(planes):
            pair(k, slot)
        if n + 1 > 3:
            for h in range(split):
                receive(n + 1, h)
        elif n + 1 == 3:
            receive_when(outer, 3)
        slot = take(n + 1)
        for k in range(planes):
            pair(k, slot)
    if teams > 1:
        slot = take_partner(teams - 1)
    for k in reversed(range(planes)):
        if teams > 1:
            pair(k, slot)
        if k:
            grad_out[k - 1] = gradient(k).astype(jnp.bfloat16)
            to_owner[k].start()
    total = gradient(0)
    for k in reversed(range(1, planes)):
        to_owner[k].wait_recv()
        total += grad_in[k - 1].astype(jnp.float32)
    out_ref[...] = total
    for copy in to_plane[1:] + [to_partner] + to_owner[1:]:
        copy.wait_send()
    for h in range(split):
        for step in (1, -1):
            @pl.when(can_go(step))
            def _():
                own_copy(step, h).wait_send()
        for n in range(1, teams):
            relay(n, h).wait_send()

            @pl.when(can_go(order[n][1]))
            def _():
                forward(n, h).wait_send()


def local(planes, teams, features, left_vectors, right_vectors):
    rows, feat = features.shape
    kind = jnp.bfloat16
    dma = pltpu.SemaphoreType.DMA
    tile, split = min(rows, 256), 2
    return pl.pallas_call(
        functools.partial(kernel, planes, teams, tile, split),
        out_shape=jax.ShapeDtypeStruct((rows, feat), jnp.float32),
        in_specs=[pl.BlockSpec(memory_space=pl.ANY)] * 3,
        out_specs=pl.BlockSpec(memory_space=pltpu.VMEM),
        scratch_shapes=[
            pltpu.VMEM((3, rows, feat), kind),
            pltpu.VMEM((max(planes - 1, 1), 3, rows, feat), kind),
            pltpu.VMEM((2 * teams, 3, rows, feat), kind),
            pltpu.VMEM((planes, rows, 2 * feat), kind),
            pltpu.VMEM((2 * teams, rows, 2 * feat), kind),
            pltpu.VMEM((planes, rows, 2 * feat), jnp.float32),
            pltpu.VMEM((max(planes - 1, 1), rows, feat), kind),
            pltpu.VMEM((max(planes - 1, 1), rows, feat), kind),
            dma((3,)),
            dma((planes,)), dma((planes,)),
            dma((teams + 1, split)), dma((teams, split)),
            dma((teams, split)), dma((teams, split)),
            dma((planes,)), dma((planes,)),
        ],
        compiler_params=pltpu.CompilerParams(collective_id=0, has_side_effects=True),
    )(features, left_vectors, right_vectors)


def solution(mesh):
    spec = P(("blk", "team"), None)
    planes, teams = mesh.shape["blk"] // 2, mesh.shape["team"]
    return jax.shard_map(
        functools.partial(local, planes, teams), mesh=mesh,
        in_specs=(spec, spec, spec), out_specs=spec, check_vma=False,
    )
```

```python
import functools
import math

import jax
import jax.numpy as jnp
from jax import lax
from jax.experimental import pallas as pl
from jax.experimental.pallas import tpu as pltpu
from jax.sharding import PartitionSpec as P

MESH = pl.DeviceIdType.MESH
LOG2E = math.log2(math.e)
RATE = math.sqrt(5.0) * LOG2E
GAIN = -(5.0 / 3.0) / LOG2E
NT = (((1,), (1,)), ((), ()))


def flip(index, bits):
    step = 1
    while step <= bits:
        if bits & step:
            index = index + step - 2 * step * ((index // step) % 2)
        step *= 2
    return index


def columns(norm, lane, first, ones):
    high = norm.astype(jnp.bfloat16).astype(jnp.float32)
    rest = norm - high
    mid = rest.astype(jnp.bfloat16).astype(jnp.float32)
    low = rest - mid
    out = jnp.where((lane >= ones) & (lane < ones + 3), 1.0, 0.0)
    for place, term in enumerate((high, mid, low)):
        out = jnp.where(lane == first + place, term, out)
    return out.astype(jnp.bfloat16)


def kernel(
    planes, teams, tile, split, x_hbm, l_hbm, r_hbm, out_ref, grad_in,
    own, tgt, src, tgt_aug, src_aug, acc, grad_out, mine_out, out_sem,
    load_sem, tgt_send, tgt_recv, z_send, z_recv, p_send, p_recv, g_send, g_recv,
):
    blk, team = lax.axis_index("blk"), lax.axis_index("team")
    plane, core = blk // 2, blk % 2
    rows, feat = x_hbm.shape

    loads = [
        pltpu.make_async_copy(ref, own.at[i], load_sem.at[i])
        for i, ref in enumerate((x_hbm, l_hbm, r_hbm))
    ]
    for load in loads:
        load.start()

    partner = (plane * 2 + 1 - core, team)
    plane_peer = [(flip(plane, k) * 2 + core, team) for k in range(planes)]
    peers = [partner] + plane_peer[1:]
    barrier = pltpu.get_barrier_semaphore()
    for peer in peers:
        pl.semaphore_signal(barrier, inc=1, device_id=peer, device_id_type=MESH)
    for step in (1, -1):
        @pl.when((team + step >= 0) & (team + step < teams))
        def _():
            pl.semaphore_signal(barrier, inc=1, device_id=(blk, team + step), device_id_type=MESH)

    def remote(source, target, send, recv, peer):
        return pltpu.make_async_remote_copy(
            src_ref=source, dst_ref=target, send_sem=send, recv_sem=recv,
            device_id=peer, device_id_type=MESH,
        )

    to_plane = [None] + [
        remote(own, tgt.at[k - 1], tgt_send.at[k], tgt_recv.at[k], plane_peer[k])
        for k in range(1, planes)
    ]
    size = rows // split
    left, right = team, teams - 1 - team
    both = jnp.minimum(left, right)

    def position(n):
        paired = n <= 2 * both
        far = jnp.where(paired, (n + 1) // 2, n - both)
        sign = jnp.where(paired, 1 - 2 * (n % 2), jnp.where(left < right, 1, -1))
        return team + sign * far, -sign

    order = [None] + [position(n) for n in range(1, teams)]

    def part_of(ref, h):
        return ref.at[:, pl.ds(h * size, size)]

    def line_copy(source, shard, h, send, step):
        return remote(
            part_of(source, h), part_of(src.at[2 * shard], h), send, z_recv.at[shard, h],
            (blk, team + step),
        )

    def can_go(step):
        return (team + step >= 0) & (team + step < teams)

    def own_copy(step, h):
        return line_copy(own, team, h, z_send.at[team if step > 0 else teams, h], step)

    def forward(n, h):
        shard, step = order[n]
        return line_copy(src.at[2 * shard], shard, h, z_send.at[shard, h], step)

    def relay(n, h):
        shard = order[n][0]
        return remote(
            part_of(src.at[2 * shard], h), part_of(src.at[2 * shard + 1], h),
            p_send.at[shard, h], p_recv.at[shard, h], partner,
        )

    mine = 2 * team
    to_partner = remote(own, src.at[mine + 1], p_send.at[team, 0], p_recv.at[team, 0], partner)
    to_owner = [None] + [
        remote(grad_out.at[k - 1], grad_in.at[k - 1], g_send.at[k], g_recv.at[k], plane_peer[k])
        for k in range(1, planes)
    ]

    for load in loads:
        load.wait()
    on_line = jnp.minimum(team, 1) + jnp.minimum(teams - 1 - team, 1)
    pl.semaphore_wait(barrier, len(peers) + on_line)
    to_partner.start()
    for h in range(split):
        for step in (1, -1):
            @pl.when(can_go(step))
            def _():
                own_copy(step, h).start()
    for k in range(1, planes):
        to_plane[k].start()

    def norm_of(x):
        xf = x.astype(jnp.float32)
        return jnp.sum(xf * xf, axis=1, keepdims=True)


    def raw_target(k):
        return own if k == 0 else tgt.at[k - 1]

    def raw_source(s):
        return own if s is mine else src.at[s]

    lane = lax.broadcasted_iota(jnp.int32, (rows, feat), 1)

    def prepare_target(k):
        x = raw_target(k)[0]
        tgt_aug[k, :, :feat] = x * jnp.bfloat16(-2.0)
        tgt_aug[k, :, feat:] = columns(norm_of(x), lane, 0, 3)

    def prepare_source(s):
        x = raw_source(s)[0]
        src_aug[s, :, :feat] = x
        src_aug[s, :, feat:] = columns(norm_of(x), lane, 3, 0)

    def tile_pair(k, s, i, j, first):
        ti, sj = pl.ds(i, tile), pl.ds(j, tile)
        target, source = raw_target(k), raw_source(s)
        src_a = src_aug[s, sj, :]
        dist = lax.dot_general(tgt_aug[k, ti, :], src_a, NT, preferred_element_type=jnp.float32)
        couple = lax.dot_general(
            jnp.concatenate([target[1, ti, :], target[2, ti, :]], axis=1),
            jnp.concatenate([source[2, sj, :], source[1, sj, :]], axis=1),
            NT, preferred_element_type=jnp.float32,
        )
        dist = jnp.maximum(dist, 1e-30)
        power = dist * lax.rsqrt(dist) * (-RATE)
        weight = ((LOG2E - power) * jnp.exp2(power) * couple).astype(jnp.bfloat16)
        part = jnp.dot(weight, src_a, preferred_element_type=jnp.float32)
        if first:
            acc[k, ti, :] = part
        else:
            acc[k, ti, :] += part

    def pair(k, s):
        if rows == tile:
            tile_pair(k, s, 0, 0, s is mine)
            return

        @pl.loop(0, rows // tile)
        def _(i):
            i = pl.multiple_of(i * tile, tile)
            tile_pair(k, s, i, 0, s is mine)

            @pl.loop(1, rows // tile)
            def _(j):
                tile_pair(k, s, i, pl.multiple_of(j * tile, tile), False)

    def gradient(k):
        total = acc[k]
        x = raw_target(k)[0].astype(jnp.float32)
        return GAIN * (total[:, feat:feat + 1] * x - total[:, :feat])

    inner = both > 0

    def receive(n, h):
        line_copy(own, order[n][0], h, z_send.at[0, 0], 0).wait_recv()

        @pl.when(can_go(order[n][1]))
        def _():
            forward(n, h).start()
        relay(n, h).start()

    def receive_when(condition, n, halves=range(split)):
        if n < teams:
            @pl.when(condition)
            def _():
                for h in halves:
                    receive(n, h)

    def take(n):
        prepare_source(2 * order[n][0])
        return 2 * order[n][0]

    def take_partner(n):
        for h in range(split):
            relay(n, h).wait_recv()
        prepare_source(2 * order[n][0] + 1)
        return 2 * order[n][0] + 1

    prepare_target(0)
    prepare_source(mine)
    pair(0, mine)
    to_partner.wait_recv()
    next_door = mine + 1
    prepare_source(next_door)
    pair(0, next_door)
    if teams > 1:
        for h in range(split):
            receive(1, h)
        receive_when(inner, 2)
        first = take(1)
        pair(0, first)
    for k in range(1, planes):
        to_plane[k].wait_recv()
        if k == planes - 1:
            receive_when(inner, 3)
        prepare_target(k)
        pair(k, mine)
        pair(k, next_door)
        if teams > 1:
            pair(k, first)
    outer = jnp.logical_not(inner)
    receive_when(outer, 2)
    for n in range(1, teams - 1):
        slot = take_partner(n)
        for k in range(planes):
            pair(k, slot)
        if n + 1 > 3:
            for h in range(split):
                receive(n + 1, h)
        elif n + 1 == 3:
            receive_when(outer, 3)
        slot = take(n + 1)
        for k in range(planes):
            pair(k, slot)
    if teams > 1:
        slot = take_partner(teams - 1)
    for k in reversed(range(planes)):
        if teams > 1:
            pair(k, slot)
        if k:
            grad_out[k - 1] = gradient(k).astype(jnp.bfloat16)
            to_owner[k].start()
    mine_out[...] = gradient(0)
    put = pltpu.make_async_copy(mine_out, out_ref, out_sem)
    put.start()
    for k in reversed(range(1, planes)):
        to_owner[k].wait_recv()
    put.wait()
    for copy in to_plane[1:] + [to_partner] + to_owner[1:]:
        copy.wait_send()
    for h in range(split):
        for step in (1, -1):
            @pl.when(can_go(step))
            def _():
                own_copy(step, h).wait_send()
        for n in range(1, teams):
            relay(n, h).wait_send()

            @pl.when(can_go(order[n][1]))
            def _():
                forward(n, h).wait_send()


def local(planes, teams, features, left_vectors, right_vectors):
    rows, feat = features.shape
    kind = jnp.bfloat16
    dma = pltpu.SemaphoreType.DMA
    tile, split = min(rows, 256), 2
    partial, received = pl.pallas_call(
        functools.partial(kernel, planes, teams, tile, split),
        out_shape=(
            jax.ShapeDtypeStruct((rows, feat), jnp.float32),
            jax.ShapeDtypeStruct((max(planes - 1, 1), rows, feat), kind),
        ),
        in_specs=[pl.BlockSpec(memory_space=pl.ANY)] * 3,
        out_specs=(pl.BlockSpec(memory_space=pl.ANY),) * 2,
        scratch_shapes=[
            pltpu.VMEM((3, rows, feat), kind),
            pltpu.VMEM((max(planes - 1, 1), 3, rows, feat), kind),
            pltpu.VMEM((2 * teams, 3, rows, feat), kind),
            pltpu.VMEM((planes, rows, 2 * feat), kind),
            pltpu.VMEM((2 * teams, rows, 2 * feat), kind),
            pltpu.VMEM((planes, rows, 2 * feat), jnp.float32),
            pltpu.VMEM((max(planes - 1, 1), rows, feat), kind),
            pltpu.VMEM((rows, feat), jnp.float32),
            dma,
            dma((3,)),
            dma((planes,)), dma((planes,)),
            dma((teams + 1, split)), dma((teams, split)),
            dma((teams, split)), dma((teams, split)),
            dma((planes,)), dma((planes,)),
        ],
        compiler_params=pltpu.CompilerParams(collective_id=0, has_side_effects=True),
    )(features, left_vectors, right_vectors)
    for k in range(planes - 1):
        partial = partial + received[k].astype(jnp.float32)
    return partial


def solution(mesh):
    spec = P(("blk", "team"), None)
    planes, teams = mesh.shape["blk"] // 2, mesh.shape["team"]
    return jax.shard_map(
        functools.partial(local, planes, teams), mesh=mesh,
        in_specs=(spec, spec, spec), out_specs=spec, check_vma=False,
    )
```
